512 devices in a mesh: tok: 64 (over y_lo, z, core), head: 8 (over y_hi, x).
Axes of the slice: x: 4, y: 8 (y_hi: 2, y_lo: 4; y = y_hi * 4 + y_lo), z: 8, core: 2. Of those that a mesh axis runs over, the one named last changes fastest.
Arguments:
- queries: bfloat16 [65536, 4096], P(('tok', 'head')), may hold values from -60 to 60
- key_states: bfloat16 [65536, 1024], P(('tok', 'head')), may hold values from -60 to 60
- value_states: bfloat16 [65536, 1024], P(('tok', 'head')), may hold values from -6 to 6
- query_gain: float32 [128], replicated, may hold values from 0.5 to 6
- key_gain: float32 [128], replicated, may hold values from 0.5 to 6
- lengths: int32 [32], replicated, may hold values from 1 to 4096, as said below
- slot_order: int32 [64, 96], P('tok'), may hold values from 0 to 95, each once within a row
Outputs:
- attention: bfloat16 [65536, 4096], P('tok', 'head')
- page_pool: bfloat16 [6144, 16, 8, 256], P('tok', None, 'head')
The draws below stay inside these ranges and needn't reach their ends.
Inputs may be any that keep to these rules, and one draw needn't show every extreme that they name: `lengths`: they sum to 65536; the first is 8 and the second exactly 4096. `slot_order`: each row is a permutation of the 96 slots.
All inputs are finite; a program needn't handle non-finite values.
Results may differ from the reference program's by a relative error of at most 0.0044.
The reference program's roundings to bfloat16 on the way (of `q_rot`, `k_rot` and `weights`) count: a program that leaves them out, or rounds other values in their place, can miss the bound.
Values may be sent and summed in bfloat16 or wider, within the bound.
A program may use at most 64 MiB of HBM per device.

```python
import math
import jax
import jax.numpy as jnp
from jax import lax

HEADS = 32
KV_HEADS = 8
HEAD_DIM = 128
REACH = 4
PAGE = 16
SHARD = 1024
TOKENS = 65536
MOST = 4096
SEGS = 32
POOL = 96
N_TOK = 64


def row_scaled(own, width):
    sample = jax.random.normal(jax.random.fold_in(own, 1), (TOKENS, width), jnp.float32)
    scales = jnp.exp(jax.random.uniform(jax.random.fold_in(own, 2), (TOKENS, 1), jnp.float32, math.log(0.5), math.log(5.0)))
    return sample * scales


def draw_queries(key, part):
    width = HEADS * HEAD_DIM
    own = jax.random.fold_in(key, 1000)
    sample = row_scaled(own, width)
    return jnp.clip(sample, -60.0, 60.0).astype(jnp.bfloat16)


def draw_key_states(key, part):
    width = KV_HEADS * HEAD_DIM
    own = jax.random.fold_in(key, 2000)
    sample = row_scaled(own, width)
    return jnp.clip(sample, -60.0, 60.0).astype(jnp.bfloat16)


def gain_draw(own):
    sample = jnp.exp(jax.random.uniform(jax.random.fold_in(own, 1), (HEAD_DIM,), jnp.float32, math.log(0.5), math.log(2.0)))
    return sample.astype(jnp.float32)


def draw_query_gain(key, part):
    return gain_draw(jax.random.fold_in(key, 3000))


def draw_key_gain(key, part):
    return gain_draw(jax.random.fold_in(key, 4000))


def draw_lengths(key, part):
    others = SEGS - 2
    extra = TOKENS - MOST - PAGE // 2 - others
    power = jax.random.randint(jax.random.fold_in(key, 5000), (others,), 0, 5).astype(jnp.int32)
    weight = jnp.left_shift(jnp.ones((others,), jnp.int32), power)
    room = MOST - 1
    share = jnp.minimum(extra * weight // jnp.sum(weight), room).astype(jnp.int32)
    remain = (extra - jnp.sum(share)).astype(jnp.int32)

    def fill_one(index, carry):
        shares, left = carry
        added = jnp.minimum(room - shares[index], left)
        return (shares.at[index].add(added), left - added)
    share, remain = lax.fori_loop(0, others, fill_one, (share, remain))
    leading = jnp.array([PAGE // 2, MOST], jnp.int32)
    return jnp.concatenate([leading, 1 + share]).astype(jnp.int32)


def level_of(stream_key, extent, cuts, low, top_value):
    loudness, own = 1.0, jax.random.fold_in(stream_key, 6)
    for dim, parts in cuts:
        heights = jnp.exp(jax.random.uniform(jax.random.fold_in(own, dim), (parts,), jnp.float32, low / len(cuts), top_value / len(cuts)))
        loudness = loudness * jnp.repeat(heights, extent[dim] // parts).reshape([-1 if axis == dim else 1 for axis in range(len(extent))])
    return loudness


def scatter_about(own_key, shape, spread, reach, split=(), kind=jnp.bfloat16):
    values = jax.random.normal(own_key, shape, jnp.float32) * spread
    if len(split) > 0:
        values = level_of(own_key, shape, split, -0.22, 0.18) * values
    return jnp.clip(values, min=-reach, max=reach).astype(kind)


def setup_inputs(seed: int = 0) -> dict:
    splits = jax.random.split(jax.random.key(seed), 8)
    queries = draw_queries(jax.random.fold_in(splits[7], 71), 0)
    key_states = draw_key_states(jax.random.fold_in(splits[7], 71), 0)
    value_states = scatter_about(splits[2], (TOKENS, KV_HEADS * HEAD_DIM), 1.0, 6.0, ((0, 512),))
    query_gain = draw_query_gain(jax.random.fold_in(splits[7], 71), 0)
    key_gain = draw_key_gain(jax.random.fold_in(splits[7], 71), 0)
    lengths = draw_lengths(jax.random.fold_in(splits[7], 71), 0)
    slot_order = jax.vmap(lambda own: jax.random.permutation(own, POOL))(jax.random.split(splits[6], N_TOK)).reshape((N_TOK, POOL)).astype(jnp.int32)
    return {"queries": queries, "key_states": key_states, "value_states": value_states, "query_gain": query_gain, "key_gain": key_gain, "lengths": lengths, "slot_order": slot_order}


def seg_table(lengths):
    seg_ends = jnp.cumsum(lengths).astype(jnp.int32)
    seg_starts = (seg_ends - lengths).astype(jnp.int32)
    return (seg_starts, seg_ends)

def locate(points, seg_starts, seg_ends):
    segment = lax.optimization_barrier(jnp.sum((points[:, None] >= seg_starts[None, :]).astype(jnp.int32), axis=1)) - 1
    onehot = segment[:, None] == jnp.arange(seg_starts.shape[0], dtype=jnp.int32)[None, :]
    first = lax.optimization_barrier(jnp.sum(jnp.where(onehot, seg_starts[None, :], 0), axis=1)).astype(jnp.int32)
    finish = lax.optimization_barrier(jnp.sum(jnp.where(onehot, seg_ends[None, :], 0), axis=1)).astype(jnp.int32)
    return (segment.astype(jnp.int32), first, finish)

def rms_scale(tensor, gain_vec):
    power_mean = lax.optimization_barrier(jnp.mean(tensor * tensor, axis=-1, keepdims=True))
    return tensor * lax.rsqrt(power_mean + 1e-06) * gain_vec

def rotary(tensor, offset):
    half_dim = tensor.shape[-1] // 2
    frequency = jnp.exp(jnp.arange(half_dim, dtype=jnp.float32) * (-2.0 * math.log(1000000.0) / tensor.shape[-1]))
    angles = offset.astype(jnp.float32)[:, None] * frequency[None, :]
    cosine = jnp.concatenate([jnp.cos(angles), jnp.cos(angles)], axis=-1)[:, None, :]
    sine_rows = jnp.concatenate([jnp.sin(angles), jnp.sin(angles)], axis=-1)[:, None, :]
    turned = jnp.concatenate([-tensor[..., half_dim:], tensor[..., :half_dim]], axis=-1)
    return tensor * cosine + turned * sine_rows

def reference(queries, key_states, value_states, query_gain, key_gain, lengths, slot_order):
    head_dim = HEAD_DIM
    group_size = HEADS // KV_HEADS
    seg_starts, seg_ends = seg_table(lengths)
    points = jnp.arange(TOKENS, dtype=jnp.int32)
    segment, first, finish = locate(points, seg_starts, seg_ends)
    offset = points - first
    q_rot = rotary(rms_scale(queries.astype(jnp.float32).reshape(TOKENS, HEADS, head_dim), query_gain), offset).astype(jnp.bfloat16)
    k_rot = rotary(rms_scale(key_states.astype(jnp.float32).reshape(TOKENS, KV_HEADS, head_dim), key_gain), offset).astype(jnp.bfloat16)
    v_all = value_states.reshape(TOKENS, KV_HEADS, head_dim)
    margin = REACH * SHARD
    span_len = (REACH + 1) * SHARD
    k_pad = jnp.concatenate([jnp.zeros((margin, KV_HEADS, head_dim), jnp.bfloat16), k_rot], axis=0)
    v_pad = jnp.concatenate([jnp.zeros((margin, KV_HEADS, head_dim), jnp.bfloat16), v_all], axis=0)
    seg_pad = jnp.concatenate([jnp.full((margin,), -1, jnp.int32), segment], axis=0)
    score_scale = 1.0 / math.sqrt(head_dim)

    def one_shard(shard_index):
        row_first = (shard_index * SHARD).astype(jnp.int32)
        q_part = lax.dynamic_slice_in_dim(q_rot, row_first, SHARD, 0).reshape(SHARD, KV_HEADS, group_size, head_dim)
        k_part = lax.dynamic_slice_in_dim(k_pad, row_first, span_len, 0)
        v_part = lax.dynamic_slice_in_dim(v_pad, row_first, span_len, 0)
        seg_keys = lax.dynamic_slice_in_dim(seg_pad, row_first, span_len, 0)
        seg_query = lax.dynamic_slice_in_dim(segment, row_first, SHARD, 0)
        query_pos = row_first + jnp.arange(SHARD, dtype=jnp.int32)
        key_pos = row_first - margin + jnp.arange(span_len, dtype=jnp.int32)
        visible = (seg_query[:, None] == seg_keys[None, :]) & (key_pos[None, :] <= query_pos[:, None])

        def one_group(group_index):
            q_group = lax.dynamic_index_in_dim(q_part, group_index, 1, keepdims=False)
            k_group = lax.dynamic_index_in_dim(k_part, group_index, 1, keepdims=False)
            v_group = lax.dynamic_index_in_dim(v_part, group_index, 1, keepdims=False)
            scores = jnp.einsum('qrd,kd->qrk', q_group.astype(jnp.float32), k_group.astype(jnp.float32)) * score_scale
            scores = jnp.where(visible[:, None, :], scores, -1e+30)
            top_row = lax.optimization_barrier(jnp.max(scores, axis=-1, keepdims=True))
            expo = jnp.where(visible[:, None, :], jnp.exp(scores - top_row), 0.0)
            denom = lax.optimization_barrier(jnp.sum(expo, axis=-1))
            weights = expo.astype(jnp.bfloat16)
            mixed = jnp.einsum('qrk,kd->qrd', weights.astype(jnp.float32), v_group.astype(jnp.float32))
            return mixed / denom[..., None]
        per_group = lax.map(one_group, jnp.arange(KV_HEADS, dtype=jnp.int32))
        return jnp.transpose(per_group, (1, 0, 2, 3)).reshape(SHARD, HEADS * head_dim).astype(jnp.bfloat16)
    attention = lax.map(one_shard, jnp.arange(N_TOK, dtype=jnp.int32)).reshape(TOKENS, HEADS * head_dim)
    page_last = jnp.minimum(first + (offset // PAGE + 1) * PAGE, finish) - 1
    page_ends = (offset % PAGE == PAGE - 1) | (points == finish - 1)
    flags = page_ends.astype(jnp.int32)
    before = jnp.cumsum(flags).astype(jnp.int32) - flags
    owner = (page_last // SHARD).astype(jnp.int32)
    rank_rows = before[page_last] - before[owner * SHARD]
    page_id = owner * POOL + slot_order[owner, rank_rows]
    target = page_id * PAGE + offset % PAGE
    paired = jnp.concatenate([k_rot, v_all], axis=-1)
    page_pool = jnp.zeros((N_TOK * POOL * PAGE, KV_HEADS, 2 * head_dim), jnp.bfloat16).at[target].set(paired)
    page_pool = page_pool.reshape(N_TOK * POOL, PAGE, KV_HEADS, 2 * head_dim)
    return (attention, page_pool)
```

```python
import functools
import math

import jax
import jax.numpy as jnp
import numpy as np
from jax import lax
from jax.experimental import pallas as pl
from jax.experimental.pallas import tpu as pltpu
from jax.sharding import PartitionSpec as P

D = 128
REACH = 4
PAGE = 16
GROUP = 4
PEERS = 8
FAR = -1e30
MESH = pl.DeviceIdType.MESH
NT = (((1,), (1,)), ((), ()))


def kernel(
    n_tok,
    q_hbm,
    k_hbm,
    v_hbm,
    qg_ref,
    kg_ref,
    freq_ref,
    len_ref,
    slot_ref,
    out_hbm,
    pool_hbm,
    qin,
    kin,
    vin,
    kvs,
    qs,
    kv,
    qbuf,
    augk,
    augq,
    acc,
    peak,
    ostage,
    pstage,
    in_sem,
    own_sem,
    out_sem,
    kv_send,
    kv_recv,
    q_send,
    q_recv,
    z_send,
    z_recv,
    s_send,
    s_recv,
):
    rows = kin.shape[0]
    shard = rows * PEERS
    half = shard // 2
    segs = len_ref.shape[0]
    tok = lax.axis_index("tok")
    head = lax.axis_index("head")
    hi, x = head // 4, lax.rem(head, 4)
    core = lax.rem(tok, 2)
    sibling = tok + 1 - 2 * core
    base = tok * shard

    def dest(n):
        return (hi if n < 4 else 1 - hi) * 4 + lax.rem(x - n + 8, 4)

    def origin(n):
        return lax.rem(hi + n // 4, 2) * 4 + lax.rem(x + n, 4)

    def rows_of(chunk):
        return pl.ds(pl.multiple_of(chunk * rows, rows), rows)

    barrier = pltpu.get_barrier_semaphore()
    for n in range(1, PEERS):
        pl.semaphore_signal(barrier, device_id=(tok, dest(n)), device_id_type=MESH)
    pl.semaphore_signal(barrier, device_id=(sibling, head), device_id_type=MESH)

    @pl.when(tok + 2 < n_tok)
    def _():
        pl.semaphore_signal(barrier, device_id=(tok + 2, head), device_id_type=MESH)

    @pl.when(tok >= 2)
    def _():
        pl.semaphore_signal(barrier, device_id=(tok - 2, head), device_id_type=MESH)

    loads = [
        pltpu.make_async_copy(k_hbm, kin, in_sem.at[0]),
        pltpu.make_async_copy(v_hbm, vin, in_sem.at[1]),
        pltpu.make_async_copy(q_hbm, qin, in_sem.at[2]),
    ]
    for load in loads:
        load.start()

    lane = lax.broadcasted_iota(jnp.int32, (1, D), 1)
    starts = jnp.full((1, D), 1 << 30, jnp.int32)
    ends = starts
    total = jnp.int32(0)
    for s in range(segs):
        starts = jnp.where(lane == s, total, starts)
        total = total + len_ref[s]
        ends = jnp.where(lane == s, total, ends)

    place = base + head * rows + lax.broadcasted_iota(jnp.int32, (rows, 1), 0)
    inside = (place >= starts) & (place < ends)
    first = jnp.sum(jnp.where(inside, starts.astype(jnp.float32), 0.0), axis=1, keepdims=True)
    angle = (place.astype(jnp.float32) - first) * freq_ref[...]
    cosine = jnp.cos(angle)
    sine = jnp.sin(angle)
    sine = jnp.where(lax.broadcasted_iota(jnp.int32, (rows, D), 1) < D // 2, -sine, sine)

    def rotated(tensor, gain):
        tensor = tensor.astype(jnp.float32)
        power = jnp.mean(tensor * tensor, axis=1, keepdims=True)
        tensor = tensor * lax.rsqrt(power + 1e-6) * gain
        return (tensor * cosine + pltpu.roll(tensor, D // 2, 1) * sine).astype(jnp.bfloat16)

    loads[0].wait()
    for g in range(PEERS):
        kvs[g, 0] = rotated(kin[:, g * D : (g + 1) * D], kg_ref[...])
    loads[1].wait()
    for g in range(PEERS):
        kvs[g, 1] = vin[:, g * D : (g + 1) * D]

    pl.semaphore_wait(
        barrier,
        PEERS + (tok >= 2).astype(jnp.int32) + (tok + 2 < n_tok).astype(jnp.int32),
    )

    own_rows = pl.ds(pl.multiple_of(REACH * shard + head * rows, rows), rows)
    kv_copies = [pltpu.make_async_copy(kvs.at[head], kv.at[:, own_rows], own_sem.at[0])]
    q_copies = [pltpu.make_async_copy(qs.at[head], qbuf.at[0], own_sem.at[1])]
    for n in range(1, PEERS):
        kv_copies.append(
            pltpu.make_async_remote_copy(
                src_ref=kvs.at[dest(n)],
                dst_ref=kv.at[:, own_rows],
                send_sem=kv_send.at[n],
                recv_sem=kv_recv.at[n],
                device_id=(tok, dest(n)),
                device_id_type=MESH,
            )
        )
        q_copies.append(
            pltpu.make_async_remote_copy(
                src_ref=qs.at[dest(n)],
                dst_ref=qbuf.at[n],
                send_sem=q_send.at[n],
                recv_sem=q_recv.at[n],
                device_id=(tok, dest(n)),
                device_id_type=MESH,
            )
        )
    for n in (4, 5, 6, 7, 1, 2, 3, 0):
        kv_copies[n].start()

    loads[2].wait()

    def turn_queries(g, carry):
        for r in range(GROUP):
            cols = pl.ds(pl.multiple_of((g * GROUP + r) * D, D), D)
            qs[g, r * rows : (r + 1) * rows] = rotated(qin[:, cols], qg_ref[...])
        return carry

    lax.fori_loop(0, PEERS, turn_queries, 0)

    def slot_rows(d, part):
        return pl.ds(pl.multiple_of((REACH - d) * shard + part * half, half), half)

    parts = (hi, 1 - hi)

    def along(src_slot, dst_slot, which, index):
        return pltpu.make_async_remote_copy(
            src_ref=kv.at[:, slot_rows(src_slot, parts[which])],
            dst_ref=kv.at[:, slot_rows(dst_slot, parts[which])],
            send_sem=z_send.at[index],
            recv_sem=z_recv.at[index],
            device_id=(tok + 2, head),
            device_id_type=MESH,
        )

    def across(src_slot, dst_slot, which, index):
        return pltpu.make_async_remote_copy(
            src_ref=kv.at[:, slot_rows(src_slot, parts[which])],
            dst_ref=kv.at[:, slot_rows(dst_slot, parts[which])],
            send_sem=s_send.at[index],
            recv_sem=s_recv.at[index],
            device_id=(sibling, head),
            device_id_type=MESH,
        )

    def give(own, which):
        @pl.when(tok + 2 < n_tok)
        def _():
            if own:
                along(0, 2, which, which).start()
            else:

                @pl.when(tok >= 2)
                def _():
                    along(2, 4, which, 2 + which).start()

        if own:

            @pl.when(core == 0)
            def _():
                across(0, 1, which, which).start()
        else:

            @pl.when((core == 0) & (tok >= 2))
            def _():
                across(2, 3, which, 2 + which).start()

            @pl.when((core == 1) & (tok >= 2))
            def _():
                across(2, 1, which, which).start()

    for d in range(1, REACH + 1):

        @pl.when(tok < d)
        def _(d=d):
            kv[:, (REACH - d) * shard : (REACH - d + 1) * shard] = jnp.zeros((2, shard, D), jnp.bfloat16)

    for n in (1, 2, 3):
        q_copies[n].start()
    q_copies[0].start()
    for n in (1, 2, 3):
        kv_copies[n].wait_recv()
    kv_copies[0].wait()
    give(True, 0)
    for n in (4, 5, 6, 7):
        kv_copies[n].wait_recv()
    give(True, 1)
    for n in (4, 5, 6, 7):
        q_copies[n].start()

    def mark_keys(index, carry):
        point = base - REACH * shard + index * rows + lax.broadcasted_iota(jnp.int32, (rows, 1), 0)
        within = (point >= starts) & (point < ends)
        augk[rows_of(index)] = jnp.where(within, 0.0, FAR).astype(jnp.bfloat16)
        return carry

    lax.fori_loop(0, (REACH + 1) * PEERS, mark_keys, 0)

    def mark_queries(index, carry):
        point = base + index * rows + lax.broadcasted_iota(jnp.int32, (rows, 1), 0)
        within = (point >= starts) & (point < ends)
        augq[rows_of(index)] = jnp.where(within, 1.0, 0.0).astype(jnp.bfloat16)
        return carry

    lax.fori_loop(0, PEERS, mark_queries, 0)

    scale = math.log2(math.e) / math.sqrt(D)

    def tile(n, begin, length, opening):
        chunk = origin(n)
        mark = augq[rows_of(chunk)]
        query = jnp.concatenate([qbuf[n], jnp.concatenate([mark] * GROUP, axis=0)], axis=1)
        at = pl.ds(pl.multiple_of(chunk * rows + begin, rows), length)
        key = jnp.concatenate([kv[0, at], augk[at]], axis=1)
        value = jnp.concatenate([kv[1, at], jnp.ones((length, D), jnp.bfloat16)], axis=1)
        score = lax.dot_general(query, key, NT, preferred_element_type=jnp.float32)
        if opening:
            query_row = lax.rem(lax.broadcasted_iota(jnp.int32, score.shape, 0), rows)
            key_row = lax.broadcasted_iota(jnp.int32, score.shape, 1)
            score = jnp.where(key_row <= query_row, score, FAR)
        top = jnp.broadcast_to(jnp.max(score, axis=1, keepdims=True), (GROUP * rows, D))
        if not opening:
            old = peak[n]
            top = jnp.maximum(old, top)
        if length >= D:
            wide = jnp.concatenate([top] * (length // D), axis=1)
        else:
            wide = top[:, :length]
        expo = jnp.exp2((score - wide) * scale).astype(jnp.bfloat16)
        mixed = jnp.dot(expo, value, preferred_element_type=jnp.float32)
        if opening:
            acc[n] = mixed
        else:
            factor = jnp.exp2((old - top) * scale)
            acc[n] = acc[n] * jnp.concatenate([factor, factor], axis=1) + mixed
        peak[n] = top

    def tiles(low, high, begin, length, opening=False):
        def step(n, carry):
            tile(n, begin, length, opening)
            return carry

        lax.fori_loop(low, high, step, 0)

    def finish(n):
        done = acc[n]
        done = (done[:, :D] / done[:, D:]).astype(jnp.bfloat16)
        for r in range(GROUP):
            ostage[n, :, r * D : (r + 1) * D] = done[r * rows : (r + 1) * rows]

    def out_copy(n):
        return pltpu.make_async_copy(ostage.at[n], out_hbm.at[rows_of(origin(n))], out_sem.at[n])

    q_copies[0].wait()
    for n in (1, 2, 3):
        q_copies[n].wait_recv()
    tiles(0, 4, REACH * shard, rows, True)

    for which in (0, 1):

        @pl.when(tok >= 2)
        def _(which=which):
            along(0, 2, which, which).wait_recv()

        give(False, which)

    for which in (0, 1):

        @pl.when(tok >= 1)
        def _(which=which):
            across(0, 1, which, which).wait_recv()

    width = shard + 128
    spot = lax.broadcasted_iota(jnp.int32, (1, width), 1)
    point = base + spot - jnp.where(spot < shard, 0, width)
    begun = jnp.zeros((1, width), jnp.int32)
    ended = begun
    paged = begun
    total = jnp.int32(0)
    pages = jnp.int32(0)
    origin_rank = jnp.int32(0)
    for s in range(segs):
        length = len_ref[s]
        after = point >= total
        begun = jnp.where(after, total, begun)
        ended = jnp.where(after, total + length, ended)
        paged = jnp.where(after, pages, paged)
        origin_rank = jnp.where(base >= total, pages + lax.shift_right_logical(jnp.maximum(base - total, 0), 4), origin_rank)
        total = total + length
        pages = pages + lax.shift_right_logical(length + (PAGE - 1), 4)
    offset = jnp.maximum(point - begun, 0)
    block = lax.shift_right_logical(offset, 4)
    last = jnp.minimum(begun + (block + 1) * PAGE, ended) - 1
    owned = (point >= 0) & (last >= base) & (last < base + shard)
    wanted = jnp.where(owned, (paged + block - origin_rank) * PAGE + (offset & (PAGE - 1)), -1)

    pool_rows = pstage.shape[0]
    piece = 256
    slots = slot_ref[...]
    ranks = lax.broadcasted_iota(jnp.int32, slots.shape, 1).astype(jnp.float32)

    def fill(index, carry):
        row = index * piece + lax.broadcasted_iota(jnp.int32, (piece, 1), 0)
        rank = jnp.sum(jnp.where(slots == lax.shift_right_logical(row, 4), ranks, 0.0), axis=1, keepdims=True)
        code = rank.astype(jnp.int32) * PAGE + (row & (PAGE - 1))
        pick = jnp.where(code == wanted, 1.0, 0.0).astype(jnp.bfloat16)
        own = pl.ds(REACH * shard, shard)
        tail = pl.ds(REACH * shard - 128, 128)
        to = pl.ds(pl.multiple_of(index * piece, piece), piece)
        for plane in (0, 1):
            rowset = jnp.concatenate([kv[plane, own], kv[plane, tail]], axis=0)
            got = jnp.dot(pick, rowset, preferred_element_type=jnp.float32)
            pstage[to, plane * D : (plane + 1) * D] = got.astype(jnp.bfloat16)
        return carry

    lax.fori_loop(0, pool_rows // piece, fill, 0)
    pool_copy = pltpu.make_async_copy(pstage, pool_hbm, own_sem.at[2])
    pool_copy.start()

    tiles(0, 4, 3 * shard, shard)
    tiles(0, 4, 2 * shard, shard)

    for which in (0, 1):

        @pl.when(tok >= 4)
        def _(which=which):
            along(2, 4, which, 2 + which).wait_recv()

        @pl.when((core == 1) & (tok >= 4))
        def _(which=which):
            across(4, 3, which, 2 + which).start()

    for which in (0, 1):

        @pl.when(tok >= 3)
        def _(which=which):
            across(2, 3, which, 2 + which).wait_recv()

    def rest(n, carry):
        tile(n, 1 * shard, shard, False)
        tile(n, 0, shard, False)
        finish(n)
        out_copy(n).start()
        return carry

    lax.fori_loop(0, 4, rest, 0)

    for n in (4, 5, 6, 7):
        q_copies[n].wait_recv()

    def whole(n, carry):
        tile(n, REACH * shard, rows, True)
        lax.fori_loop(0, 4, lambda j, c: (tile(n, (3 - j) * shard, shard, False), c)[1], 0)
        finish(n)
        out_copy(n).start()
        return carry

    lax.fori_loop(4, 8, whole, 0)

    for n in range(1, PEERS):
        kv_copies[n].wait_send()
        q_copies[n].wait_send()
    for which in (0, 1):

        @pl.when(tok + 2 < n_tok)
        def _(which=which):
            along(0, 2, which, which).wait_send()

            @pl.when(tok >= 2)
            def _():
                along(2, 4, which, 2 + which).wait_send()

        @pl.when((core == 0) | (tok >= 2))
        def _(which=which):
            across(0, 1, which, which).wait_send()

        @pl.when(((core == 0) & (tok >= 2)) | ((core == 1) & (tok >= 4)))
        def _(which=which):
            across(2, 3, which, 2 + which).wait_send()

    for n in range(PEERS):
        out_copy(n).wait()
    pool_copy.wait()


def on_device(queries, key_states, value_states, query_gain, key_gain, lengths, slot_order):
    rows = queries.shape[0]
    shard = rows * PEERS
    slots = slot_order.shape[1]
    frequency = np.exp(np.arange(D // 2) * (-2.0 * math.log(1000000.0) / D)).astype(np.float32)
    frequency = jnp.asarray(np.concatenate([frequency, frequency])[None, :])
    vmem = pl.BlockSpec(memory_space=pltpu.VMEM)
    smem = pl.BlockSpec(memory_space=pltpu.SMEM)
    anywhere = pl.BlockSpec(memory_space=pl.ANY)
    bf16 = jnp.bfloat16
    dma = pltpu.SemaphoreType.DMA
    attention, pool = pl.pallas_call(
        functools.partial(kernel, lax.axis_size("tok")),
        out_shape=(
            jax.ShapeDtypeStruct((shard, GROUP * D), bf16),
            jax.ShapeDtypeStruct((slots * PAGE, 2 * D), bf16),
        ),
        in_specs=[anywhere, anywhere, anywhere, vmem, vmem, vmem, smem, vmem],
        out_specs=(anywhere, anywhere),
        scratch_shapes=[
            pltpu.VMEM((rows, PEERS * GROUP * D), bf16),
            pltpu.VMEM((rows, PEERS * D), bf16),
            pltpu.VMEM((rows, PEERS * D), bf16),
            pltpu.VMEM((PEERS, 2, rows, D), bf16),
            pltpu.VMEM((PEERS, GROUP * rows, D), bf16),
            pltpu.VMEM((2, (REACH + 1) * shard, D), bf16),
            pltpu.VMEM((PEERS, GROUP * rows, D), bf16),
            pltpu.VMEM(((REACH + 1) * shard, D), bf16),
            pltpu.VMEM((shard, D), bf16),
            pltpu.VMEM((PEERS, GROUP * rows, 2 * D), jnp.float32),
            pltpu.VMEM((PEERS, GROUP * rows, D), jnp.float32),
            pltpu.VMEM((PEERS, rows, GROUP * D), bf16),
            pltpu.VMEM((slots * PAGE, 2 * D), bf16),
            dma((3,)),
            dma((3,)),
            dma((PEERS,)),
            dma((PEERS,)),
            dma((PEERS,)),
            dma((PEERS,)),
            dma((PEERS,)),
            dma((4,)),
            dma((4,)),
            dma((4,)),
            dma((4,)),
        ],
        compiler_params=pltpu.CompilerParams(
            collective_id=0, has_side_effects=True, vmem_limit_bytes=56 * 2**20
        ),
        name="paged_prefill",
    )(
        queries,
        key_states,
        value_states,
        query_gain[None, :],
        key_gain[None, :],
        frequency,
        lengths,
        slot_order,
    )
    return attention, pool.reshape(slots, PAGE, 1, 2 * D)


def solution(mesh):
    in_specs = (
        P(("tok", "head"), None),
        P(("tok", "head"), None),
        P(("tok", "head"), None),
        P(),
        P(),
        P(),
        P("tok", None),
    )
    out_specs = (P("tok", "head"), P("tok", None, "head", None))
    return jax.shard_map(
        on_device, mesh=mesh, in_specs=in_specs, out_specs=out_specs, check_vma=False
    )
```

```python
import functools
import math

import jax
import jax.numpy as jnp
import numpy as np
from jax import lax
from jax.experimental import pallas as pl
from jax.experimental.pallas import tpu as pltpu
from jax.sharding import PartitionSpec as P

D = 128
REACH = 4
PAGE = 16
GROUP = 4
PEERS = 8
FAR = -1e30
MESH = pl.DeviceIdType.MESH
NT = (((1,), (1,)), ((), ()))
FAR_SENDS = (4, 5, 6, 7)


def kernel(
    n_tok,
    q_hbm,
    k_hbm,
    v_hbm,
    qg_ref,
    kg_ref,
    freq_ref,
    len_ref,
    slot_ref,
    out_hbm,
    pool_hbm,
    qin,
    kin,
    vin,
    kvs,
    qs,
    kv,
    qbuf,
    kv_relay,
    q_relay,
    augk,
    augq,
    acc,
    total_ref,
    peak,
    ostage,
    pstage,
    in_sem,
    own_sem,
    out_sem,
    kv_send,
    kv_recv,
    q_send,
    q_recv,
    kv_on,
    kv_mid,
    q_on,
    q_mid,
    z_send,
    z_recv,
    s_send,
    s_recv,
):
    rows = kin.shape[0]
    shard = rows * PEERS
    half = shard // 2
    segs = len_ref.shape[0]
    tok = lax.axis_index("tok")
    head = lax.axis_index("head")
    hi, x = head // 4, lax.rem(head, 4)
    core = lax.rem(tok, 2)
    sibling = tok + 1 - 2 * core
    base = tok * shard

    run = n_tok // 4
    y = hi * 4 + tok // run
    at_run = lax.rem(tok, run)
    ending = at_run >= run - 2
    ahead = (at_run >= run - 4) & (at_run < run - 2) & (tok + 4 < n_tok)
    opened = (at_run < 2) & (tok >= 4)

    def device(col, row):
        row = lax.rem(row + 8, 8)
        return (lax.rem(row, 4) * run + at_run, row // 4 * 4 + lax.rem(col + 8, 4))

    def dest(n):
        return (hi if n < 4 else 1 - hi) * 4 + lax.rem(x - n + 8, 4)

    def origin(n):
        return lax.rem(hi + n // 4, 2) * 4 + lax.rem(x + n, 4)

    def way(n):
        return 2 if n % 2 == 0 else -2

    crossing = at_run >= run - 4

    def query_way(n):
        return jnp.where(crossing, -2, 2) if n == 6 else way(n)

    def rows_of(chunk):
        return pl.ds(pl.multiple_of(chunk * rows, rows), rows)

    barrier = pltpu.get_barrier_semaphore()

    def greet(where):
        pl.semaphore_signal(barrier, device_id=where, device_id_type=MESH)

    for n in (1, 2, 3):
        greet((tok, dest(n)))
    for n in FAR_SENDS:
        greet(device(x - n, y + way(n)))
        greet(device(x + n, y - way(n)))
    greet(device(x - 6, y - way(6)))
    greet(device(x + 6, y + way(6)))
    greet(device(x, y + 2))
    greet(device(x, y - 2))
    greet((sibling, head))

    @pl.when(tok + 2 < n_tok)
    def _():
        greet((tok + 2, head))

    @pl.when(tok >= 2)
    def _():
        greet((tok - 2, head))

    @pl.when(ahead)
    def _():
        greet((tok + 4, head))

    @pl.when(opened)
    def _():
        greet((tok - 4, head))

    loads = [
        pltpu.make_async_copy(k_hbm, kin, in_sem.at[0]),
        pltpu.make_async_copy(v_hbm, vin, in_sem.at[1]),
        pltpu.make_async_copy(q_hbm, qin, in_sem.at[2]),
    ]
    for load in loads:
        load.start()

    lane = lax.broadcasted_iota(jnp.int32, (1, D), 1)
    starts = jnp.full((1, D), 1 << 30, jnp.int32)
    ends = starts
    total = jnp.int32(0)
    for s in range(segs):
        starts = jnp.where(lane == s, total, starts)
        total = total + len_ref[s]
        ends = jnp.where(lane == s, total, ends)

    place = base + head * rows + lax.broadcasted_iota(jnp.int32, (rows, 1), 0)
    inside = (place >= starts) & (place < ends)
    first = jnp.sum(jnp.where(inside, starts.astype(jnp.float32), 0.0), axis=1, keepdims=True)
    angle = (place.astype(jnp.float32) - first) * freq_ref[...]
    cosine = jnp.cos(angle)
    sine = jnp.sin(angle)
    sine = jnp.where(lax.broadcasted_iota(jnp.int32, (rows, D), 1) < D // 2, -sine, sine)

    def rotated(tensor, gain):
        tensor = tensor.astype(jnp.float32)
        power = jnp.mean(tensor * tensor, axis=1, keepdims=True)
        tensor = tensor * lax.rsqrt(power + 1e-6) * gain
        return (tensor * cosine + pltpu.roll(tensor, D // 2, 1) * sine).astype(jnp.bfloat16)

    loads[0].wait()
    for g in range(PEERS):
        kvs[g, 0] = rotated(kin[:, g * D : (g + 1) * D], kg_ref[...])
    loads[1].wait()
    for g in range(PEERS):
        kvs[g, 1] = vin[:, g * D : (g + 1) * D]

    guests = (tok >= 2, tok + 2 < n_tok, ahead, opened)
    pl.semaphore_wait(barrier, 16 + sum(g.astype(jnp.int32) for g in guests))

    def own_rows(head_index):
        return pl.ds(pl.multiple_of(REACH * shard + head_index * rows, rows), rows)

    def remote(source, target, send, recv, where):
        return pltpu.make_async_remote_copy(
            src_ref=source,
            dst_ref=target,
            send_sem=send,
            recv_sem=recv,
            device_id=where,
            device_id_type=MESH,
        )

    kv_copies = [pltpu.make_async_copy(kvs.at[head], kv.at[:, own_rows(head)], own_sem.at[0])]
    q_copies = [pltpu.make_async_copy(qs.at[head], qbuf.at[0], own_sem.at[1])]
    for n in (1, 2, 3):
        where = (tok, dest(n))
        kv_copies.append(
            remote(kvs.at[dest(n)], kv.at[:, own_rows(head)], kv_send.at[n], kv_recv.at[n], where)
        )
        q_copies.append(remote(qs.at[dest(n)], qbuf.at[n], q_send.at[n], q_recv.at[n], where))
    kv_passes, q_passes = {}, {}
    for n in FAR_SENDS:
        k = n - 4
        where = device(x - n, y + way(n))
        kv_copies.append(remote(kvs.at[dest(n)], kv_relay.at[k], kv_send.at[n], kv_mid.at[k], where))
        there = device(x - n, y + query_way(n))
        q_copies.append(remote(qs.at[dest(n)], q_relay.at[k], q_send.at[n], q_mid.at[k], there))
        where = device(x, y + way(n))
        origin_head = device(x + n, y - way(n))[1]
        kv_passes[n] = remote(
            kv_relay.at[k], kv.at[:, own_rows(origin_head)], kv_on.at[k], kv_recv.at[n], where
        )
        there = device(x, y + query_way(n))
        q_passes[n] = remote(q_relay.at[k], qbuf.at[n], q_on.at[k], q_recv.at[n], there)
    for n in (4, 5, 6, 7, 1, 2, 3, 0):
        kv_copies[n].start()

    loads[2].wait()

    def turn_queries(n, carry):
        g = lax.rem(hi + n // 4, 2) * 4 + lax.rem(x - n + 8, 4)
        for r in range(GROUP):
            cols = pl.ds(pl.multiple_of((g * GROUP + r) * D, D), D)
            qs[g, r * rows : (r + 1) * rows] = rotated(qin[:, cols], qg_ref[...])
        return carry

    def slot_rows(d, part):
        return pl.ds(pl.multiple_of((REACH - d) * shard + part * half, half), half)

    parts = (hi, 1 - hi)

    def along(src_slot, dst_slot, which, index):
        return remote(
            kv.at[:, slot_rows(src_slot, parts[which])],
            kv.at[:, slot_rows(dst_slot, parts[which])],
            z_send.at[index],
            z_recv.at[dst_slot - 2 + which],
            (tok + (dst_slot - src_slot), head),
        )

    def across(src_slot, dst_slot, which):
        index = dst_slot - 1 + which
        return remote(
            kv.at[:, slot_rows(src_slot, parts[which])],
            kv.at[:, slot_rows(dst_slot, parts[which])],
            s_send.at[index],
            s_recv.at[index],
            (sibling, head),
        )

    def along_own(which):
        return along(0, 2, which, which)

    def along_on(which):
        return along(2, 4, which, 2 + which)

    def along_far(which):
        return along(0, 4, which, 4 + which)

    has_next = tok + 2 < n_tok
    passes = has_next & (tok >= 2) & jnp.logical_not(ending)

    def give_own(which):
        @pl.when(has_next)
        def _():
            along_own(which).start()

        @pl.when(ahead)
        def _():
            along_far(which).start()

        @pl.when(core == 0)
        def _():
            across(0, 1, which).start()

    def give_on(which):
        @pl.when(passes)
        def _():
            along_on(which).start()

        @pl.when((core == 1) & (tok >= 2))
        def _():
            across(2, 1, which).start()

        @pl.when((core == 0) & (tok >= 2))
        def _():
            across(2, 3, which).start()

    for d in range(1, REACH + 1):

        @pl.when(tok < d)
        def _(d=d):
            kv[:, (REACH - d) * shard : (REACH - d + 1) * shard] = jnp.zeros((2, shard, D), jnp.bfloat16)

    straight = jnp.logical_not(crossing)
    late = at_run < 2

    def pass_queries(n):
        q_copies[n].wait_recv()
        q_passes[n].start()

    def halo_on(which):
        @pl.when(tok >= 2)
        def _():
            along_own(which).wait_recv()

        give_on(which)

    lax.fori_loop(4, 6, turn_queries, 0)

    @pl.when(straight)
    def _():
        q_copies[4].start()
        q_copies[5].start()

    for n in (1, 2, 3):
        kv_copies[n].wait_recv()
    kv_copies[0].wait()
    give_own(0)
    for n in FAR_SENDS:
        kv_copies[n].wait_recv()
        kv_passes[n].start()
    lax.fori_loop(6, 8, turn_queries, 0)

    @pl.when(straight)
    def _():
        q_copies[6].start()
        q_copies[7].start()

    lax.fori_loop(0, 4, turn_queries, 0)
    for n in (1, 2, 3, 0):
        q_copies[n].start()

    @pl.when(jnp.logical_not(late))
    def _():
        halo_on(0)

    def mark_keys(index, carry):
        point = base - REACH * shard + index * rows + lax.broadcasted_iota(jnp.int32, (rows, 1), 0)
        within = (point >= starts) & (point < ends)
        augk[rows_of(index)] = jnp.where(within, 0.0, FAR).astype(jnp.bfloat16)
        return carry

    lax.fori_loop(0, (REACH + 1) * PEERS, mark_keys, 0)

    def mark_queries(index, carry):
        point = base + index * rows + lax.broadcasted_iota(jnp.int32, (rows, 1), 0)
        within = (point >= starts) & (point < ends)
        augq[rows_of(index)] = jnp.where(within, 1.0, 0.0).astype(jnp.bfloat16)
        return carry

    lax.fori_loop(0, PEERS, mark_queries, 0)

    for n in FAR_SENDS:
        kv_passes[n].wait_recv()
    give_own(1)

    @pl.when(crossing)
    def _():
        for n in FAR_SENDS:
            q_copies[n].start()
        halo_on(1)

    for n in FAR_SENDS:
        pass_queries(n)

    @pl.when(late)
    def _():
        halo_on(0)

    @pl.when(straight)
    def _():
        halo_on(1)

    scale = math.log2(math.e) / math.sqrt(D)

    def attend(n, begins, opening, closing):
        chunk = origin(n)
        mark = augq[rows_of(chunk)]
        query = jnp.concatenate([qbuf[n], jnp.concatenate([mark] * GROUP, axis=0)], axis=1)
        runs = [(begin, shard) for begin in begins]
        if opening:
            runs = [(REACH * shard, rows)] + runs

        def keys_at(index):
            begin, length = runs[index]
            return pl.ds(pl.multiple_of(chunk * rows + begin, rows), length)

        def front(index):
            at = keys_at(index)
            key = jnp.concatenate([kv[0, at], augk[at]], axis=1)
            score = lax.dot_general(query, key, NT, preferred_element_type=jnp.float32)
            if opening and index == 0:
                query_row = lax.rem(lax.broadcasted_iota(jnp.int32, score.shape, 0), rows)
                key_row = lax.broadcasted_iota(jnp.int32, score.shape, 1)
                score = jnp.where(key_row <= query_row, score, FAR)
            return score, jnp.broadcast_to(jnp.max(score, axis=1, keepdims=True), (GROUP * rows, D))

        ready = front(0)
        old = None if opening else peak[n]
        for index, (_, length) in enumerate(runs):
            score, top = ready
            if index + 1 < len(runs):
                ready = front(index + 1)
            if old is not None:
                top = jnp.maximum(old, top)
            expo = jnp.exp2((score - jnp.concatenate([top] * (length // D), axis=1)) * scale)
            part = expo[:, :D]
            for piece in range(1, length // D):
                part = part + expo[:, piece * D : (piece + 1) * D]
            mixed = jnp.dot(
                expo.astype(jnp.bfloat16), kv[1, keys_at(index)], preferred_element_type=jnp.float32
            )
            if old is None:
                acc[n] = mixed
                total_ref[n] = part
            else:
                factor = jnp.exp2((old - top) * scale)
                acc[n] = acc[n] * factor + mixed
                total_ref[n] = total_ref[n] * factor + part
            old = top
        if closing:
            done = acc[n] / jnp.sum(total_ref[n], axis=1, keepdims=True)
            done = done.astype(jnp.bfloat16)
            for r in range(GROUP):
                ostage[n, :, r * D : (r + 1) * D] = done[r * rows : (r + 1) * rows]
            out_copy(n).start()
        else:
            peak[n] = old

    def out_copy(n):
        return pltpu.make_async_copy(ostage.at[n], out_hbm.at[rows_of(origin(n))], out_sem.at[n])

    q_copies[0].wait()
    for n in (1, 2, 3):
        q_copies[n].wait_recv()

    for which in (0, 1):

        @pl.when(tok >= 1)
        def _(which=which):
            across(0, 1, which).wait_recv()

    def near_first(n, carry):
        attend(n, (3 * shard, 2 * shard), True, False)

        return carry

    lax.fori_loop(0, 4, near_first, 0)

    width = shard + 128
    spot = lax.broadcasted_iota(jnp.int32, (1, width), 1)
    point = base + spot - jnp.where(spot < shard, 0, width)
    begun = jnp.zeros((1, width), jnp.int32)
    ended = begun
    paged = begun
    total = jnp.int32(0)
    pages = jnp.int32(0)
    origin_rank = jnp.int32(0)
    for s in range(segs):
        length = len_ref[s]
        after = point >= total
        begun = jnp.where(after, total, begun)
        ended = jnp.where(after, total + length, ended)
        paged = jnp.where(after, pages, paged)
        origin_rank = jnp.where(base >= total, pages + lax.shift_right_logical(jnp.maximum(base - total, 0), 4), origin_rank)
        total = total + length
        pages = pages + lax.shift_right_logical(length + (PAGE - 1), 4)
    offset = jnp.maximum(point - begun, 0)
    block = lax.shift_right_logical(offset, 4)
    last = jnp.minimum(begun + (block + 1) * PAGE, ended) - 1
    owned = (point >= 0) & (last >= base) & (last < base + shard)
    wanted = jnp.where(owned, (paged + block - origin_rank) * PAGE + (offset & (PAGE - 1)), -1)

    pool_rows = pstage.shape[0]
    piece = 256
    slots = slot_ref[...]
    ranks = lax.broadcasted_iota(jnp.int32, slots.shape, 1).astype(jnp.float32)

    def fill(index, carry):
        row = index * piece + lax.broadcasted_iota(jnp.int32, (piece, 1), 0)
        rank = jnp.sum(jnp.where(slots == lax.shift_right_logical(row, 4), ranks, 0.0), axis=1, keepdims=True)
        code = rank.astype(jnp.int32) * PAGE + (row & (PAGE - 1))
        pick = jnp.where(code == wanted, 1.0, 0.0).astype(jnp.bfloat16)
        own = pl.ds(REACH * shard, shard)
        tail = pl.ds(REACH * shard - 128, 128)
        to = pl.ds(pl.multiple_of(index * piece, piece), piece)
        for plane in (0, 1):
            rowset = jnp.concatenate([kv[plane, own], kv[plane, tail]], axis=0)
            got = jnp.dot(pick, rowset, preferred_element_type=jnp.float32)
            pstage[to, plane * D : (plane + 1) * D] = got.astype(jnp.bfloat16)
        return carry

    lax.fori_loop(0, pool_rows // piece, fill, 0)
    pool_copy = pltpu.make_async_copy(pstage, pool_hbm, own_sem.at[2])
    pool_copy.start()

    for which in (0, 1):

        @pl.when(tok >= 4)
        def _(which=which):
            along_on(which).wait_recv()

        @pl.when((core == 1) & (tok >= 4))
        def _(which=which):
            across(4, 3, which).start()

    for which in (0, 1):

        @pl.when(tok >= 3)
        def _(which=which):
            across(2, 3, which).wait_recv()

    def near_last(n, carry):
        attend(n, (shard, 0), False, True)
        return carry

    lax.fori_loop(0, 4, near_last, 0)

    def far(n, carry):
        remote(q_relay.at[0], qbuf.at[n], q_on.at[0], q_recv.at[n], (sibling, head)).wait_recv()
        attend(n, (3 * shard, 2 * shard, shard, 0), True, True)
        return carry

    lax.fori_loop(4, PEERS, far, 0)

    for n in range(1, PEERS):
        kv_copies[n].wait_send()
        q_copies[n].wait_send()
    for n in FAR_SENDS:
        kv_passes[n].wait_send()
        q_passes[n].wait_send()
    for which in (0, 1):

        @pl.when(has_next)
        def _(which=which):
            along_own(which).wait_send()

        @pl.when(passes)
        def _(which=which):
            along_on(which).wait_send()

        @pl.when(ahead)
        def _(which=which):
            along_far(which).wait_send()

        @pl.when((core == 0) | (tok >= 2))
        def _(which=which):
            across(0, 1, which).wait_send()

        @pl.when(((core == 0) & (tok >= 2)) | ((core == 1) & (tok >= 4)))
        def _(which=which):
            across(2, 3, which).wait_send()

    for n in range(PEERS):
        out_copy(n).wait()
    pool_copy.wait()


def on_device(queries, key_states, value_states, query_gain, key_gain, lengths, slot_order):
    rows = queries.shape[0]
    shard = rows * PEERS
    slots = slot_order.shape[1]
    frequency = np.exp(np.arange(D // 2) * (-2.0 * math.log(1000000.0) / D)).astype(np.float32)
    frequency = jnp.asarray(np.concatenate([frequency, frequency])[None, :])
    vmem = pl.BlockSpec(memory_space=pltpu.VMEM)
    smem = pl.BlockSpec(memory_space=pltpu.SMEM)
    anywhere = pl.BlockSpec(memory_space=pl.ANY)
    bf16 = jnp.bfloat16
    dma = pltpu.SemaphoreType.DMA
    attention, pool = pl.pallas_call(
        functools.partial(kernel, lax.axis_size("tok")),
        out_shape=(
            jax.ShapeDtypeStruct((shard, GROUP * D), bf16),
            jax.ShapeDtypeStruct((slots * PAGE, 2 * D), bf16),
        ),
        in_specs=[anywhere, anywhere, anywhere, vmem, vmem, vmem, smem, vmem],
        out_specs=(anywhere, anywhere),
        scratch_shapes=[
            pltpu.VMEM((rows, PEERS * GROUP * D), bf16),
            pltpu.VMEM((rows, PEERS * D), bf16),
            pltpu.VMEM((rows, PEERS * D), bf16),
            pltpu.VMEM((PEERS, 2, rows, D), bf16),
            pltpu.VMEM((PEERS, GROUP * rows, D), bf16),
            pltpu.VMEM((2, (REACH + 1) * shard, D), bf16),
            pltpu.VMEM((PEERS, GROUP * rows, D), bf16),
            pltpu.VMEM((4, 2, rows, D), bf16),
            pltpu.VMEM((4, GROUP * rows, D), bf16),
            pltpu.VMEM(((REACH + 1) * shard, D), bf16),
            pltpu.VMEM((shard, D), bf16),
            pltpu.VMEM((PEERS, GROUP * rows, D), jnp.float32),
            pltpu.VMEM((PEERS, GROUP * rows, D), jnp.float32),
            pltpu.VMEM((PEERS, GROUP * rows, D), jnp.float32),
            pltpu.VMEM((PEERS, rows, GROUP * D), bf16),
            pltpu.VMEM((slots * PAGE, 2 * D), bf16),
            dma((3,)),
            dma((3,)),
            dma((PEERS,)),
            dma((PEERS,)),
            dma((PEERS,)),
            dma((PEERS,)),
            dma((PEERS,)),
            dma((4,)),
            dma((4,)),
            dma((4,)),
            dma((4,)),
            dma((6,)),
            dma((4,)),
            dma((4,)),
            dma((4,)),
        ],
        compiler_params=pltpu.CompilerParams(
            collective_id=0, has_side_effects=True, vmem_limit_bytes=56 * 2**20
        ),
        name="paged_prefill",
    )(
        queries,
        key_states,
        value_states,
        query_gain[None, :],
        key_gain[None, :],
        frequency,
        lengths,
        slot_order,
    )
    return attention, pool.reshape(slots, PAGE, 1, 2 * D)


def solution(mesh):
    in_specs = (
        P(("tok", "head"), None),
        P(("tok", "head"), None),
        P(("tok", "head"), None),
        P(),
        P(),
        P(),
        P("tok", None),
    )
    out_specs = (P("tok", "head"), P("tok", None, "head", None))
    return jax.shard_map(
        on_device, mesh=mesh, in_specs=in_specs, out_specs=out_specs, check_vma=False
    )
```

```python
import functools
import math

import jax
import jax.numpy as jnp
import numpy as np
from jax import lax
from jax.experimental import pallas as pl
from jax.experimental.pallas import tpu as pltpu
from jax.sharding import PartitionSpec as P

D = 128
REACH = 4
PAGE = 16
GROUP = 4
PEERS = 8
FAR = -1e30
MESH = pl.DeviceIdType.MESH
NT = (((1,), (1,)), ((), ()))
FAR_SENDS = (4, 5, 6, 7)


def kernel(
    n_tok,
    q_hbm,
    k_hbm,
    v_hbm,
    qg_ref,
    kg_ref,
    freq_ref,
    len_ref,
    slot_ref,
    out_hbm,
    pool_hbm,
    qin,
    kin,
    vin,
    kvs,
    qs,
    kv,
    qbuf,
    kv_relay,
    q_relay,
    halo_relay,
    augk,
    augq,
    acc,
    total_ref,
    peak,
    ostage,
    pstage,
    in_sem,
    own_sem,
    out_sem,
    kv_send,
    kv_recv,
    q_send,
    q_recv,
    kv_on,
    kv_mid,
    q_on,
    q_mid,
    z_send,
    z_recv,
    turn_send,
    turn_recv,
    s_send,
    s_recv,
):
    rows = kin.shape[0]
    shard = rows * PEERS
    half = shard // 2
    segs = len_ref.shape[0]
    tok = lax.axis_index("tok")
    head = lax.axis_index("head")
    hi, x = head // 4, lax.rem(head, 4)
    core = lax.rem(tok, 2)
    sibling = tok + 1 - 2 * core
    base = tok * shard

    run = n_tok // 4
    y = hi * 4 + tok // run
    at_run = lax.rem(tok, run)
    ending = at_run >= run - 2
    ahead = (at_run >= run - 4) & (at_run < run - 2) & (tok + 4 < n_tok)
    opened = (at_run < 2) & (tok >= 4)
    between = (at_run // 2 == 3) & (tok + 10 < n_tok)

    def device(col, row):
        row = lax.rem(row + 8, 8)
        return (lax.rem(row, 4) * run + at_run, row // 4 * 4 + lax.rem(col + 8, 4))

    def dest(n):
        return (hi if n < 4 else 1 - hi) * 4 + lax.rem(x - n + 8, 4)

    def origin(n):
        return lax.rem(hi + n // 4, 2) * 4 + lax.rem(x + n, 4)

    def way(n):
        return 2 if n % 2 == 0 else -2

    crossing = at_run >= run - 2

    def query_way(n):
        return jnp.where(crossing, -2, 2) if n == 6 else way(n)

    def rows_of(chunk):
        return pl.ds(pl.multiple_of(chunk * rows, rows), rows)

    barrier = pltpu.get_barrier_semaphore()

    def greet(where):
        pl.semaphore_signal(barrier, device_id=where, device_id_type=MESH)

    for n in (1, 2, 3):
        greet((tok, dest(n)))
    for n in FAR_SENDS:
        greet(device(x - n, y + way(n)))
        greet(device(x + n, y - way(n)))
    greet(device(x - 6, y - way(6)))
    greet(device(x + 6, y + way(6)))
    greet(device(x, y + 2))
    greet(device(x, y - 2))
    greet((sibling, head))

    @pl.when(tok + 2 < n_tok)
    def _():
        greet((tok + 2, head))

    @pl.when(tok >= 2)
    def _():
        greet((tok - 2, head))

    @pl.when(ahead)
    def _():
        greet((tok - 6, head))

    @pl.when(between)
    def _():
        greet((tok + 6, head))
        greet((tok + 10, head))

    @pl.when(opened)
    def _():
        greet((tok - 10, head))

    loads = [
        pltpu.make_async_copy(k_hbm, kin, in_sem.at[0]),
        pltpu.make_async_copy(v_hbm, vin, in_sem.at[1]),
        pltpu.make_async_copy(q_hbm, qin, in_sem.at[2]),
    ]
    for load in loads:
        load.start()

    lane = lax.broadcasted_iota(jnp.int32, (1, D), 1)
    starts = jnp.full((1, D), 1 << 30, jnp.int32)
    ends = starts
    total = jnp.int32(0)
    for s in range(segs):
        starts = jnp.where(lane == s, total, starts)
        total = total + len_ref[s]
        ends = jnp.where(lane == s, total, ends)

    place = base + head * rows + lax.broadcasted_iota(jnp.int32, (rows, 1), 0)
    inside = (place >= starts) & (place < ends)
    first = jnp.sum(jnp.where(inside, starts.astype(jnp.float32), 0.0), axis=1, keepdims=True)
    angle = (place.astype(jnp.float32) - first) * freq_ref[...]
    cosine = jnp.cos(angle)
    sine = jnp.sin(angle)
    sine = jnp.where(lax.broadcasted_iota(jnp.int32, (rows, D), 1) < D // 2, -sine, sine)

    def rotated(tensor, gain):
        tensor = tensor.astype(jnp.float32)
        power = jnp.mean(tensor * tensor, axis=1, keepdims=True)
        tensor = tensor * lax.rsqrt(power + 1e-6) * gain
        return (tensor * cosine + pltpu.roll(tensor, D // 2, 1) * sine).astype(jnp.bfloat16)

    loads[0].wait()
    for g in range(PEERS):
        kvs[g, 0] = rotated(kin[:, g * D : (g + 1) * D], kg_ref[...])
    loads[1].wait()
    for g in range(PEERS):
        kvs[g, 1] = vin[:, g * D : (g + 1) * D]

    guests = (tok >= 2, tok + 2 < n_tok, ahead, opened, between, between)
    pl.semaphore_wait(barrier, 16 + sum(g.astype(jnp.int32) for g in guests))

    def own_rows(head_index):
        return pl.ds(pl.multiple_of(REACH * shard + head_index * rows, rows), rows)

    def remote(source, target, send, recv, where):
        return pltpu.make_async_remote_copy(
            src_ref=source,
            dst_ref=target,
            send_sem=send,
            recv_sem=recv,
            device_id=where,
            device_id_type=MESH,
        )

    kv_copies = [pltpu.make_async_copy(kvs.at[head], kv.at[:, own_rows(head)], own_sem.at[0])]
    q_copies = [pltpu.make_async_copy(qs.at[head], qbuf.at[0], own_sem.at[1])]
    for n in (1, 2, 3):
        where = (tok, dest(n))
        kv_copies.append(
            remote(kvs.at[dest(n)], kv.at[:, own_rows(head)], kv_send.at[n], kv_recv.at[n], where)
        )
        q_copies.append(remote(qs.at[dest(n)], qbuf.at[n], q_send.at[n], q_recv.at[n], where))
    kv_passes, q_passes = {}, {}
    for n in FAR_SENDS:
        k = n - 4
        where = device(x - n, y + way(n))
        kv_copies.append(remote(kvs.at[dest(n)], kv_relay.at[k], kv_send.at[n], kv_mid.at[k], where))
        there = device(x - n, y + query_way(n))
        q_copies.append(remote(qs.at[dest(n)], q_relay.at[k], q_send.at[n], q_mid.at[k], there))
        where = device(x, y + way(n))
        origin_head = device(x + n, y - way(n))[1]
        kv_passes[n] = remote(
            kv_relay.at[k], kv.at[:, own_rows(origin_head)], kv_on.at[k], kv_recv.at[n], where
        )
        there = device(x, y + query_way(n))
        q_passes[n] = remote(q_relay.at[k], qbuf.at[n], q_on.at[k], q_recv.at[n], there)
    for n in (4, 5, 6, 7, 1, 2, 3, 0):
        kv_copies[n].start()

    loads[2].wait()

    def turn_queries(n, carry):
        g = lax.rem(hi + n // 4, 2) * 4 + lax.rem(x - n + 8, 4)
        for r in range(GROUP):
            cols = pl.ds(pl.multiple_of((g * GROUP + r) * D, D), D)
            qs[g, r * rows : (r + 1) * rows] = rotated(qin[:, cols], qg_ref[...])
        return carry

    def slot_rows(d, part):
        return pl.ds(pl.multiple_of((REACH - d) * shard + part * half, half), half)

    parts = (hi, 1 - hi)

    def along(src_slot, dst_slot, which, index):
        return remote(
            kv.at[:, slot_rows(src_slot, parts[which])],
            kv.at[:, slot_rows(dst_slot, parts[which])],
            z_send.at[index],
            z_recv.at[dst_slot - 2 + which],
            (tok + (dst_slot - src_slot), head),
        )

    def across(src_slot, dst_slot, which):
        index = dst_slot - 1 + which
        return remote(
            kv.at[:, slot_rows(src_slot, parts[which])],
            kv.at[:, slot_rows(dst_slot, parts[which])],
            s_send.at[index],
            s_recv.at[index],
            (sibling, head),
        )

    def along_own(which):
        return along(0, 2, which, which)

    def along_on(which):
        return along(2, 4, which, 2 + which)

    def far_out(which):
        return remote(
            kv.at[:, slot_rows(0, parts[which])],
            halo_relay.at[which],
            z_send.at[4 + which],
            turn_recv.at[which],
            (tok - 6, head),
        )

    def far_on(which):
        return remote(
            halo_relay.at[which],
            kv.at[:, slot_rows(4, parts[which])],
            turn_send.at[which],
            z_recv.at[2 + which],
            (tok + 10, head),
        )

    def turn(which):
        @pl.when(between)
        def _():
            far_out(which).wait_recv()
            far_on(which).start()

    has_next = tok + 2 < n_tok
    passes = has_next & (tok >= 2) & jnp.logical_not(ending)

    def give_own(which):
        @pl.when(has_next)
        def _():
            along_own(which).start()

        @pl.when(ahead)
        def _():
            far_out(which).start()

        @pl.when(core == 0)
        def _():
            across(0, 1, which).start()

    def give_on(which):
        @pl.when(passes)
        def _():
            along_on(which).start()

        @pl.when((core == 1) & (tok >= 2))
        def _():
            across(2, 1, which).start()

        @pl.when((core == 0) & (tok >= 2))
        def _():
            across(2, 3, which).start()

    for d in range(1, REACH + 1):

        @pl.when(tok < d)
        def _(d=d):
            kv[:, (REACH - d) * shard : (REACH - d + 1) * shard] = jnp.zeros((2, shard, D), jnp.bfloat16)

    straight = jnp.logical_not(crossing)
    late = at_run < 2

    def pass_queries(n):
        q_copies[n].wait_recv()
        q_passes[n].start()

    def halo_on(which):
        @pl.when(tok >= 2)
        def _():
            along_own(which).wait_recv()

        give_on(which)

    lax.fori_loop(4, 6, turn_queries, 0)

    @pl.when(straight)
    def _():
        q_copies[4].start()
        q_copies[5].start()

    for n in (1, 2, 3):
        kv_copies[n].wait_recv()
    kv_copies[0].wait()
    give_own(0)
    for n in FAR_SENDS:
        kv_copies[n].wait_recv()
        kv_passes[n].start()
    lax.fori_loop(6, 8, turn_queries, 0)

    @pl.when(straight)
    def _():
        q_copies[6].start()
        q_copies[7].start()

    lax.fori_loop(0, 4, turn_queries, 0)
    for n in (1, 2, 3, 0):
        q_copies[n].start()

    @pl.when(jnp.logical_not(late))
    def _():
        halo_on(0)

    turn(0)

    def mark_keys(index, carry):
        point = base - REACH * shard + index * rows + lax.broadcasted_iota(jnp.int32, (rows, 1), 0)
        within = (point >= starts) & (point < ends)
        augk[rows_of(index)] = jnp.where(within, 0.0, FAR).astype(jnp.bfloat16)
        return carry

    lax.fori_loop(0, (REACH + 1) * PEERS, mark_keys, 0)

    def mark_queries(index, carry):
        point = base + index * rows + lax.broadcasted_iota(jnp.int32, (rows, 1), 0)
        within = (point >= starts) & (point < ends)
        augq[rows_of(index)] = jnp.where(within, 1.0, 0.0).astype(jnp.bfloat16)
        return carry

    lax.fori_loop(0, PEERS, mark_queries, 0)

    for n in FAR_SENDS:
        kv_passes[n].wait_recv()
    give_own(1)

    @pl.when(crossing)
    def _():
        for n in FAR_SENDS:
            q_copies[n].start()
        halo_on(1)

    for n in FAR_SENDS:
        pass_queries(n)

    @pl.when(late)
    def _():
        halo_on(0)

    @pl.when(straight)
    def _():
        halo_on(1)

    turn(1)

    scale = math.log2(math.e) / math.sqrt(D)

    def attend(n, begins, opening, closing):
        chunk = origin(n)
        mark = augq[rows_of(chunk)]
        query = jnp.concatenate([qbuf[n], jnp.concatenate([mark] * GROUP, axis=0)], axis=1)
        runs = [(begin, shard) for begin in begins]
        if opening:
            runs = [(REACH * shard, rows)] + runs

        def keys_at(index):
            begin, length = runs[index]
            return pl.ds(pl.multiple_of(chunk * rows + begin, rows), length)

        def front(index):
            at = keys_at(index)
            key = jnp.concatenate([kv[0, at], augk[at]], axis=1)
            score = lax.dot_general(query, key, NT, preferred_element_type=jnp.float32)
            if opening and index == 0:
                query_row = lax.rem(lax.broadcasted_iota(jnp.int32, score.shape, 0), rows)
                key_row = lax.broadcasted_iota(jnp.int32, score.shape, 1)
                score = jnp.where(key_row <= query_row, score, FAR)
            return score, jnp.broadcast_to(jnp.max(score, axis=1, keepdims=True), (GROUP * rows, D))

        ready = front(0)
        old = None if opening else peak[n]
        for index, (_, length) in enumerate(runs):
            score, top = ready
            if index + 1 < len(runs):
                ready = front(index + 1)
            if old is not None:
                top = jnp.maximum(old, top)
            expo = jnp.exp2((score - jnp.concatenate([top] * (length // D), axis=1)) * scale)
            part = expo[:, :D]
            for piece in range(1, length // D):
                part = part + expo[:, piece * D : (piece + 1) * D]
            mixed = jnp.dot(
                expo.astype(jnp.bfloat16), kv[1, keys_at(index)], preferred_element_type=jnp.float32
            )
            if old is None:
                acc[n] = mixed
                total_ref[n] = part
            else:
                factor = jnp.exp2((old - top) * scale)
                acc[n] = acc[n] * factor + mixed
                total_ref[n] = total_ref[n] * factor + part
            old = top
        if closing:
            done = acc[n] / jnp.sum(total_ref[n], axis=1, keepdims=True)
            done = done.astype(jnp.bfloat16)
            for r in range(GROUP):
                ostage[n, :, r * D : (r + 1) * D] = done[r * rows : (r + 1) * rows]
            out_copy(n).start()
        else:
            peak[n] = old

    def out_copy(n):
        return pltpu.make_async_copy(ostage.at[n], out_hbm.at[rows_of(origin(n))], out_sem.at[n])

    q_copies[0].wait()
    for n in (1, 2, 3):
        q_copies[n].wait_recv()

    for which in (0, 1):

        @pl.when(tok >= 1)
        def _(which=which):
            across(0, 1, which).wait_recv()

    def near_first(n, carry):
        attend(n, (3 * shard, 2 * shard), True, False)

        return carry

    lax.fori_loop(0, 4, near_first, 0)

    width = shard + 128
    spot = lax.broadcasted_iota(jnp.int32, (1, width), 1)
    point = base + spot - jnp.where(spot < shard, 0, width)
    begun = jnp.zeros((1, width), jnp.int32)
    ended = begun
    paged = begun
    total = jnp.int32(0)
    pages = jnp.int32(0)
    origin_rank = jnp.int32(0)
    for s in range(segs):
        length = len_ref[s]
        after = point >= total
        begun = jnp.where(after, total, begun)
        ended = jnp.where(after, total + length, ended)
        paged = jnp.where(after, pages, paged)
        origin_rank = jnp.where(base >= total, pages + lax.shift_right_logical(jnp.maximum(base - total, 0), 4), origin_rank)
        total = total + length
        pages = pages + lax.shift_right_logical(length + (PAGE - 1), 4)
    offset = jnp.maximum(point - begun, 0)
    block = lax.shift_right_logical(offset, 4)
    last = jnp.minimum(begun + (block + 1) * PAGE, ended) - 1
    owned = (point >= 0) & (last >= base) & (last < base + shard)
    wanted = jnp.where(owned, (paged + block - origin_rank) * PAGE + (offset & (PAGE - 1)), -1)

    pool_rows = pstage.shape[0]
    piece = 256
    slots = slot_ref[...]
    ranks = lax.broadcasted_iota(jnp.int32, slots.shape, 1).astype(jnp.float32)

    def fill(index, carry):
        row = index * piece + lax.broadcasted_iota(jnp.int32, (piece, 1), 0)
        rank = jnp.sum(jnp.where(slots == lax.shift_right_logical(row, 4), ranks, 0.0), axis=1, keepdims=True)
        code = rank.astype(jnp.int32) * PAGE + (row & (PAGE - 1))
        pick = jnp.where(code == wanted, 1.0, 0.0).astype(jnp.bfloat16)
        own = pl.ds(REACH * shard, shard)
        tail = pl.ds(REACH * shard - 128, 128)
        to = pl.ds(pl.multiple_of(index * piece, piece), piece)
        for plane in (0, 1):
            rowset = jnp.concatenate([kv[plane, own], kv[plane, tail]], axis=0)
            got = jnp.dot(pick, rowset, preferred_element_type=jnp.float32)
            pstage[to, plane * D : (plane + 1) * D] = got.astype(jnp.bfloat16)
        return carry

    lax.fori_loop(0, pool_rows // piece, fill, 0)
    pool_copy = pltpu.make_async_copy(pstage, pool_hbm, own_sem.at[2])
    pool_copy.start()

    for which in (0, 1):

        @pl.when(tok >= 4)
        def _(which=which):
            along_on(which).wait_recv()

        @pl.when((core == 1) & (tok >= 4))
        def _(which=which):
            across(4, 3, which).start()

    for which in (0, 1):

        @pl.when(tok >= 3)
        def _(which=which):
            across(2, 3, which).wait_recv()

    def near_last(n, carry):
        attend(n, (shard, 0), False, True)
        return carry

    lax.fori_loop(0, 4, near_last, 0)

    def far(n, carry):
        remote(q_relay.at[0], qbuf.at[n], q_on.at[0], q_recv.at[n], (sibling, head)).wait_recv()
        attend(n, (3 * shard, 2 * shard, shard, 0), True, True)
        return carry

    lax.fori_loop(4, PEERS, far, 0)

    for n in range(1, PEERS):
        kv_copies[n].wait_send()
        q_copies[n].wait_send()
    for n in FAR_SENDS:
        kv_passes[n].wait_send()
        q_passes[n].wait_send()
    for which in (0, 1):

        @pl.when(has_next)
        def _(which=which):
            along_own(which).wait_send()

        @pl.when(passes)
        def _(which=which):
            along_on(which).wait_send()

        @pl.when(ahead)
        def _(which=which):
            far_out(which).wait_send()

        @pl.when(between)
        def _(which=which):
            far_on(which).wait_send()

        @pl.when((core == 0) | (tok >= 2))
        def _(which=which):
            across(0, 1, which).wait_send()

        @pl.when(((core == 0) & (tok >= 2)) | ((core == 1) & (tok >= 4)))
        def _(which=which):
            across(2, 3, which).wait_send()

    for n in range(PEERS):
        out_copy(n).wait()
    pool_copy.wait()


def on_device(queries, key_states, value_states, query_gain, key_gain, lengths, slot_order):
    rows = queries.shape[0]
    shard = rows * PEERS
    slots = slot_order.shape[1]
    frequency = np.exp(np.arange(D // 2) * (-2.0 * math.log(1000000.0) / D)).astype(np.float32)
    frequency = jnp.asarray(np.concatenate([frequency, frequency])[None, :])
    vmem = pl.BlockSpec(memory_space=pltpu.VMEM)
    smem = pl.BlockSpec(memory_space=pltpu.SMEM)
    anywhere = pl.BlockSpec(memory_space=pl.ANY)
    bf16 = jnp.bfloat16
    dma = pltpu.SemaphoreType.DMA
    attention, pool = pl.pallas_call(
        functools.partial(kernel, lax.axis_size("tok")),
        out_shape=(
            jax.ShapeDtypeStruct((shard, GROUP * D), bf16),
            jax.ShapeDtypeStruct((slots * PAGE, 2 * D), bf16),
        ),
        in_specs=[anywhere, anywhere, anywhere, vmem, vmem, vmem, smem, vmem],
        out_specs=(anywhere, anywhere),
        scratch_shapes=[
            pltpu.VMEM((rows, PEERS * GROUP * D), bf16),
            pltpu.VMEM((rows, PEERS * D), bf16),
            pltpu.VMEM((rows, PEERS * D), bf16),
            pltpu.VMEM((PEERS, 2, rows, D), bf16),
            pltpu.VMEM((PEERS, GROUP * rows, D), bf16),
            pltpu.VMEM((2, (REACH + 1) * shard, D), bf16),
            pltpu.VMEM((PEERS, GROUP * rows, D), bf16),
            pltpu.VMEM((4, 2, rows, D), bf16),
            pltpu.VMEM((4, GROUP * rows, D), bf16),
            pltpu.VMEM((2, 2, shard // 2, D), bf16),
            pltpu.VMEM(((REACH + 1) * shard, D), bf16),
            pltpu.VMEM((shard, D), bf16),
            pltpu.VMEM((PEERS, GROUP * rows, D), jnp.float32),
            pltpu.VMEM((PEERS, GROUP * rows, D), jnp.float32),
            pltpu.VMEM((PEERS, GROUP * rows, D), jnp.float32),
            pltpu.VMEM((PEERS, rows, GROUP * D), bf16),
            pltpu.VMEM((slots * PAGE, 2 * D), bf16),
            dma((3,)),
            dma((3,)),
            dma((PEERS,)),
            dma((PEERS,)),
            dma((PEERS,)),
            dma((PEERS,)),
            dma((PEERS,)),
            dma((4,)),
            dma((4,)),
            dma((4,)),
            dma((4,)),
            dma((6,)),
            dma((4,)),
            dma((2,)),
            dma((2,)),
            dma((4,)),
            dma((4,)),
        ],
        compiler_params=pltpu.CompilerParams(
            collective_id=0, has_side_effects=True, vmem_limit_bytes=56 * 2**20
        ),
        name="paged_prefill",
    )(
        queries,
        key_states,
        value_states,
        query_gain[None, :],
        key_gain[None, :],
        frequency,
        lengths,
        slot_order,
    )
    return attention, pool.reshape(slots, PAGE, 1, 2 * D)


def solution(mesh):
    in_specs = (
        P(("tok", "head"), None),
        P(("tok", "head"), None),
        P(("tok", "head"), None),
        P(),
        P(),
        P(),
        P("tok", None),
    )
    out_specs = (P("tok", "head"), P("tok", None, "head", None))
    return jax.shard_map(
        on_device, mesh=mesh, in_specs=in_specs, out_specs=out_specs, check_vma=False
    )
```

```python
import functools
import math

import jax
import jax.numpy as jnp
import numpy as np
from jax import lax
from jax.experimental import pallas as pl
from jax.experimental.pallas import tpu as pltpu
from jax.sharding import PartitionSpec as P

D = 128
REACH = 4
PAGE = 16
GROUP = 4
PEERS = 8
FAR = -1e30
MESH = pl.DeviceIdType.MESH
NT = (((1,), (1,)), ((), ()))
FAR_SENDS = (4, 5, 6, 7)


def kernel(
    n_tok,
    q_hbm,
    k_hbm,
    v_hbm,
    qg_ref,
    kg_ref,
    freq_ref,
    len_ref,
    slot_ref,
    out_hbm,
    pool_hbm,
    qin,
    kin,
    vin,
    kvs,
    qs,
    kv,
    qbuf,
    kv_relay,
    q_relay,
    halo_relay,
    augk,
    augq,
    acc,
    total_ref,
    peak,
    ostage,
    pstage,
    in_sem,
    own_sem,
    out_sem,
    kv_send,
    kv_recv,
    q_send,
    q_recv,
    kv_on,
    kv_mid,
    q_on,
    q_mid,
    z_send,
    z_recv,
    turn_send,
    turn_recv,
    s_send,
    s_recv,
):
    rows = kin.shape[0]
    shard = rows * PEERS
    half = shard // 2
    segs = len_ref.shape[0]
    tok = lax.axis_index("tok")
    head = lax.axis_index("head")
    hi, x = head // 4, lax.rem(head, 4)
    core = lax.rem(tok, 2)
    sibling = tok + 1 - 2 * core
    base = tok * shard

    run = n_tok // 4
    y = hi * 4 + tok // run
    at_run = lax.rem(tok, run)
    ending = at_run >= run - 2
    ahead = (at_run >= run - 4) & (at_run < run - 2) & (tok + 4 < n_tok)
    opened = (at_run < 2) & (tok >= 4)
    between = (at_run // 2 == 3) & (tok + 10 < n_tok)

    def device(col, row):
        row = lax.rem(row + 8, 8)
        return (lax.rem(row, 4) * run + at_run, row // 4 * 4 + lax.rem(col + 8, 4))

    def dest(n):
        return (hi if n < 4 else 1 - hi) * 4 + lax.rem(x - n + 8, 4)

    def origin(n):
        return lax.rem(hi + n // 4, 2) * 4 + lax.rem(x + n, 4)

    def way(n):
        return 2 if n % 2 == 0 else -2

    crossing = at_run >= run - 2

    def query_way(n):
        return jnp.where(crossing, -2, 2) if n == 6 else way(n)

    def rows_of(chunk):
        return pl.ds(pl.multiple_of(chunk * rows, rows), rows)

    barrier = pltpu.get_barrier_semaphore()

    def greet(where):
        pl.semaphore_signal(barrier, device_id=where, device_id_type=MESH)

    for n in (1, 2, 3):
        greet((tok, dest(n)))
    for n in FAR_SENDS:
        greet(device(x - n, y + way(n)))
        greet(device(x + n, y - way(n)))
    greet(device(x - 6, y - way(6)))
    greet(device(x + 6, y + way(6)))
    greet(device(x, y + 2))
    greet(device(x, y - 2))
    greet((sibling, head))

    @pl.when(tok + 2 < n_tok)
    def _():
        greet((tok + 2, head))

    @pl.when(tok >= 2)
    def _():
        greet((tok - 2, head))

    @pl.when(ahead)
    def _():
        greet((tok - 6, head))

    @pl.when(between)
    def _():
        greet((tok + 6, head))
        greet((tok + 10, head))

    @pl.when(opened)
    def _():
        greet((tok - 10, head))

    loads = [
        pltpu.make_async_copy(k_hbm, kin, in_sem.at[0]),
        pltpu.make_async_copy(v_hbm, vin, in_sem.at[1]),
        pltpu.make_async_copy(q_hbm, qin, in_sem.at[2]),
    ]
    for load in loads:
        load.start()

    lane = lax.broadcasted_iota(jnp.int32, (1, D), 1)
    starts = jnp.full((1, D), 1 << 30, jnp.int32)
    ends = starts
    total = jnp.int32(0)
    for s in range(segs):
        starts = jnp.where(lane == s, total, starts)
        total = total + len_ref[s]
        ends = jnp.where(lane == s, total, ends)

    place = base + head * rows + lax.broadcasted_iota(jnp.int32, (rows, 1), 0)
    inside = (place >= starts) & (place < ends)
    first = jnp.sum(jnp.where(inside, starts.astype(jnp.float32), 0.0), axis=1, keepdims=True)
    angle = (place.astype(jnp.float32) - first) * freq_ref[...]
    cosine = jnp.cos(angle)
    sine = jnp.sin(angle)
    sine = jnp.where(lax.broadcasted_iota(jnp.int32, (rows, D), 1) < D // 2, -sine, sine)

    def rotated(tensor, gain):
        tensor = tensor.astype(jnp.float32)
        power = jnp.mean(tensor * tensor, axis=1, keepdims=True)
        tensor = tensor * lax.rsqrt(power + 1e-6) * gain
        return (tensor * cosine + pltpu.roll(tensor, D // 2, 1) * sine).astype(jnp.bfloat16)

    loads[0].wait()
    for g in range(PEERS):
        kvs[g, 0] = rotated(kin[:, g * D : (g + 1) * D], kg_ref[...])
    loads[1].wait()
    for g in range(PEERS):
        kvs[g, 1] = vin[:, g * D : (g + 1) * D]

    guests = (tok >= 2, tok + 2 < n_tok, ahead, opened, between, between)
    pl.semaphore_wait(barrier, 16 + sum(g.astype(jnp.int32) for g in guests))

    def own_rows(head_index):
        return pl.ds(pl.multiple_of(REACH * shard + head_index * rows, rows), rows)

    def remote(source, target, send, recv, where):
        return pltpu.make_async_remote_copy(
            src_ref=source,
            dst_ref=target,
            send_sem=send,
            recv_sem=recv,
            device_id=where,
            device_id_type=MESH,
        )

    kv_copies = [pltpu.make_async_copy(kvs.at[head], kv.at[:, own_rows(head)], own_sem.at[0])]
    q_copies = [pltpu.make_async_copy(qs.at[head], qbuf.at[0], own_sem.at[1])]
    for n in (1, 2, 3):
        where = (tok, dest(n))
        kv_copies.append(
            remote(kvs.at[dest(n)], kv.at[:, own_rows(head)], kv_send.at[n], kv_recv.at[n], where)
        )
        q_copies.append(remote(qs.at[dest(n)], qbuf.at[n], q_send.at[n], q_recv.at[n], where))
    kv_passes, q_passes = {}, {}
    for n in FAR_SENDS:
        k = n - 4
        where = device(x - n, y + way(n))
        kv_copies.append(remote(kvs.at[dest(n)], kv_relay.at[k], kv_send.at[n], kv_mid.at[k], where))
        there = device(x - n, y + query_way(n))
        q_copies.append(remote(qs.at[dest(n)], q_relay.at[k], q_send.at[n], q_mid.at[k], there))
        where = device(x, y + way(n))
        origin_head = device(x + n, y - way(n))[1]
        kv_passes[n] = remote(
            kv_relay.at[k], kv.at[:, own_rows(origin_head)], kv_on.at[k], kv_recv.at[n], where
        )
        there = device(x, y + query_way(n))
        q_passes[n] = remote(q_relay.at[k], qbuf.at[n], q_on.at[k], q_recv.at[n], there)
    for n in (4, 5, 6, 7, 1, 2, 3, 0):
        kv_copies[n].start()

    loads[2].wait()

    def turn_queries(n, carry):
        g = lax.rem(hi + n // 4, 2) * 4 + lax.rem(x - n + 8, 4)
        for r in range(GROUP):
            cols = pl.ds(pl.multiple_of((g * GROUP + r) * D, D), D)
            qs[g, r * rows : (r + 1) * rows] = rotated(qin[:, cols], qg_ref[...])
        return carry

    def slot_rows(d, part):
        return pl.ds(pl.multiple_of((REACH - d) * shard + part * half, half), half)

    parts = (hi, 1 - hi)

    def along(src_slot, dst_slot, which, index):
        return remote(
            kv.at[:, slot_rows(src_slot, parts[which])],
            kv.at[:, slot_rows(dst_slot, parts[which])],
            z_send.at[index],
            z_recv.at[dst_slot - 2 + which],
            (tok + (dst_slot - src_slot), head),
        )

    def across(src_slot, dst_slot, which):
        index = dst_slot - 1 + which
        return remote(
            kv.at[:, slot_rows(src_slot, parts[which])],
            kv.at[:, slot_rows(dst_slot, parts[which])],
            s_send.at[index],
            s_recv.at[index],
            (sibling, head),
        )

    def along_own(which):
        return along(0, 2, which, which)

    def along_on(which):
        return along(2, 4, which, 2 + which)

    def far_out(which):
        return remote(
            kv.at[:, slot_rows(0, parts[which])],
            halo_relay.at[which],
            z_send.at[4 + which],
            turn_recv.at[which],
            (tok - 6, head),
        )

    def far_on(which):
        return remote(
            halo_relay.at[which],
            kv.at[:, slot_rows(4, parts[which])],
            turn_send.at[which],
            z_recv.at[2 + which],
            (tok + 10, head),
        )

    def turn(which):
        @pl.when(between)
        def _():
            far_out(which).wait_recv()
            far_on(which).start()

    has_next = tok + 2 < n_tok
    passes = has_next & (tok >= 2) & jnp.logical_not(ending)

    def give_own(which):
        @pl.when(has_next)
        def _():
            along_own(which).start()

        @pl.when(ahead)
        def _():
            far_out(which).start()

        @pl.when(core == 0)
        def _():
            across(0, 1, which).start()

    def give_on(which):
        @pl.when(passes)
        def _():
            along_on(which).start()

        @pl.when((core == 1) & (tok >= 2))
        def _():
            across(2, 1, which).start()

        @pl.when((core == 0) & (tok >= 2))
        def _():
            across(2, 3, which).start()

    for d in range(1, REACH + 1):

        @pl.when(tok < d)
        def _(d=d):
            kv[:, (REACH - d) * shard : (REACH - d + 1) * shard] = jnp.zeros((2, shard, D), jnp.bfloat16)

    straight = jnp.logical_not(crossing)
    late = at_run < 2

    def pass_queries(n):
        q_copies[n].wait_recv()
        q_passes[n].start()

    def halo_on(which):
        @pl.when(tok >= 2)
        def _():
            along_own(which).wait_recv()

        give_on(which)

    lax.fori_loop(4, 6, turn_queries, 0)

    @pl.when(straight)
    def _():
        q_copies[4].start()
        q_copies[5].start()

    for n in (1, 2, 3):
        kv_copies[n].wait_recv()
    kv_copies[0].wait()
    give_own(0)
    for n in FAR_SENDS:
        kv_copies[n].wait_recv()
        kv_passes[n].start()
    lax.fori_loop(6, 8, turn_queries, 0)

    @pl.when(straight)
    def _():
        q_copies[6].start()
        q_copies[7].start()

    lax.fori_loop(0, 4, turn_queries, 0)
    for n in (1, 2, 3, 0):
        q_copies[n].start()

    @pl.when(jnp.logical_not(late))
    def _():
        halo_on(0)

    turn(0)

    def mark_keys(index, carry):
        point = base - REACH * shard + index * rows + lax.broadcasted_iota(jnp.int32, (rows, 1), 0)
        within = (point >= starts) & (point < ends)
        augk[rows_of(index)] = jnp.where(within, 0.0, FAR).astype(jnp.bfloat16)
        return carry

    lax.fori_loop(0, (REACH + 1) * PEERS, mark_keys, 0)

    def mark_queries(index, carry):
        point = base + index * rows + lax.broadcasted_iota(jnp.int32, (rows, 1), 0)
        within = (point >= starts) & (point < ends)
        augq[rows_of(index)] = jnp.where(within, 1.0, 0.0).astype(jnp.bfloat16)
        return carry

    lax.fori_loop(0, PEERS, mark_queries, 0)

    for n in FAR_SENDS:
        kv_passes[n].wait_recv()
    give_own(1)

    @pl.when(crossing)
    def _():
        for n in FAR_SENDS:
            q_copies[n].start()
        halo_on(1)

    for n in FAR_SENDS:
        pass_queries(n)

    width = shard + 128
    spot = lax.broadcasted_iota(jnp.int32, (1, width), 1)
    point = base + spot - jnp.where(spot < shard, 0, width)
    begun = jnp.zeros((1, width), jnp.int32)
    ended = begun
    paged = begun
    total = jnp.int32(0)
    pages = jnp.int32(0)
    origin_rank = jnp.int32(0)
    for s in range(segs):
        length = len_ref[s]
        after = point >= total
        begun = jnp.where(after, total, begun)
        ended = jnp.where(after, total + length, ended)
        paged = jnp.where(after, pages, paged)
        origin_rank = jnp.where(base >= total, pages + lax.shift_right_logical(jnp.maximum(base - total, 0), 4), origin_rank)
        total = total + length
        pages = pages + lax.shift_right_logical(length + (PAGE - 1), 4)
    offset = jnp.maximum(point - begun, 0)
    block = lax.shift_right_logical(offset, 4)
    last = jnp.minimum(begun + (block + 1) * PAGE, ended) - 1
    owned = (point >= 0) & (last >= base) & (last < base + shard)
    wanted = jnp.where(owned, (paged + block - origin_rank) * PAGE + (offset & (PAGE - 1)), -1)

    pool_rows = pstage.shape[0]
    piece = 256
    slots = slot_ref[...]
    ranks = lax.broadcasted_iota(jnp.int32, slots.shape, 1).astype(jnp.float32)

    def picked(index, low, high):
        row = index * piece + lax.broadcasted_iota(jnp.int32, (piece, 1), 0)
        rank = jnp.sum(jnp.where(slots == lax.shift_right_logical(row, 4), ranks, 0.0), axis=1, keepdims=True)
        code = rank.astype(jnp.int32) * PAGE + (row & (PAGE - 1))
        return jnp.where(code == wanted[:, low:high], 1.0, 0.0).astype(jnp.bfloat16)

    def fill(index, carry):
        pick = picked(index, 0, shard)
        to = pl.ds(pl.multiple_of(index * piece, piece), piece)
        for plane in (0, 1):
            got = jnp.dot(pick, kv[plane, pl.ds(REACH * shard, shard)], preferred_element_type=jnp.float32)
            pstage[to, plane * D : (plane + 1) * D] = got.astype(jnp.bfloat16)
        return carry

    def fill_tail(index, carry):
        pick = picked(index, shard, width)
        to = pl.ds(pl.multiple_of(index * piece, piece), piece)
        for plane in (0, 1):
            cols = slice(plane * D, (plane + 1) * D)
            got = jnp.dot(pick, kv[plane, pl.ds(REACH * shard - 128, 128)], preferred_element_type=jnp.float32)
            pstage[to, cols] = pstage[to, cols] + got.astype(jnp.bfloat16)
        return carry

    lax.fori_loop(0, pool_rows // piece, fill, 0)

    @pl.when(late)
    def _():
        halo_on(0)

    @pl.when(straight)
    def _():
        halo_on(1)

    turn(1)

    scale = math.log2(math.e) / math.sqrt(D)

    def attend(n, begins, opening, closing):
        chunk = origin(n)
        mark = augq[rows_of(chunk)]
        query = jnp.concatenate([qbuf[n], jnp.concatenate([mark] * GROUP, axis=0)], axis=1)
        runs = [(begin, shard) for begin in begins]
        if opening:
            runs = [(REACH * shard, rows)] + runs

        def keys_at(index):
            begin, length = runs[index]
            return pl.ds(pl.multiple_of(chunk * rows + begin, rows), length)

        def front(index):
            at = keys_at(index)
            key = jnp.concatenate([kv[0, at], augk[at]], axis=1)
            score = lax.dot_general(query, key, NT, preferred_element_type=jnp.float32)
            if opening and index == 0:
                query_row = lax.rem(lax.broadcasted_iota(jnp.int32, score.shape, 0), rows)
                key_row = lax.broadcasted_iota(jnp.int32, score.shape, 1)
                score = jnp.where(key_row <= query_row, score, FAR)
            return score, jnp.broadcast_to(jnp.max(score, axis=1, keepdims=True), (GROUP * rows, D))

        ready = front(0)
        old = None if opening else peak[n]
        for index, (_, length) in enumerate(runs):
            score, top = ready
            if index + 1 < len(runs):
                ready = front(index + 1)
            if old is not None:
                top = jnp.maximum(old, top)
            expo = jnp.exp2((score - jnp.concatenate([top] * (length // D), axis=1)) * scale)
            part = expo[:, :D]
            for piece in range(1, length // D):
                part = part + expo[:, piece * D : (piece + 1) * D]
            mixed = jnp.dot(
                expo.astype(jnp.bfloat16), kv[1, keys_at(index)], preferred_element_type=jnp.float32
            )
            if old is None:
                acc[n] = mixed
                total_ref[n] = part
            else:
                factor = jnp.exp2((old - top) * scale)
                acc[n] = acc[n] * factor + mixed
                total_ref[n] = total_ref[n] * factor + part
            old = top
        if closing:
            done = acc[n] / jnp.sum(total_ref[n], axis=1, keepdims=True)
            done = done.astype(jnp.bfloat16)
            for r in range(GROUP):
                ostage[n, :, r * D : (r + 1) * D] = done[r * rows : (r + 1) * rows]
            out_copy(n).start()
        else:
            peak[n] = old

    def out_copy(n):
        return pltpu.make_async_copy(ostage.at[n], out_hbm.at[rows_of(origin(n))], out_sem.at[n])

    q_copies[0].wait()
    for n in (1, 2, 3):
        q_copies[n].wait_recv()

    for which in (0, 1):

        @pl.when(tok >= 1)
        def _(which=which):
            across(0, 1, which).wait_recv()

    def near_first(n, carry):
        attend(n, (3 * shard, 2 * shard), True, False)

        return carry

    lax.fori_loop(0, 4, near_first, 0)

    lax.fori_loop(0, pool_rows // piece, fill_tail, 0)
    pool_copy = pltpu.make_async_copy(pstage, pool_hbm, own_sem.at[2])
    pool_copy.start()

    for which in (0, 1):

        @pl.when(tok >= 4)
        def _(which=which):
            along_on(which).wait_recv()

        @pl.when((core == 1) & (tok >= 4))
        def _(which=which):
            across(4, 3, which).start()

    for which in (0, 1):

        @pl.when(tok >= 3)
        def _(which=which):
            across(2, 3, which).wait_recv()

    def near_last(n, carry):
        attend(n, (shard, 0), False, True)
        return carry

    lax.fori_loop(0, 4, near_last, 0)

    def far(n, carry):
        remote(q_relay.at[0], qbuf.at[n], q_on.at[0], q_recv.at[n], (sibling, head)).wait_recv()
        attend(n, (3 * shard, 2 * shard, shard, 0), True, True)
        return carry

    lax.fori_loop(4, PEERS, far, 0)

    for n in range(1, PEERS):
        kv_copies[n].wait_send()
        q_copies[n].wait_send()
    for n in FAR_SENDS:
        kv_passes[n].wait_send()
        q_passes[n].wait_send()
    for which in (0, 1):

        @pl.when(has_next)
        def _(which=which):
            along_own(which).wait_send()

        @pl.when(passes)
        def _(which=which):
            along_on(which).wait_send()

        @pl.when(ahead)
        def _(which=which):
            far_out(which).wait_send()

        @pl.when(between)
        def _(which=which):
            far_on(which).wait_send()

        @pl.when((core == 0) | (tok >= 2))
        def _(which=which):
            across(0, 1, which).wait_send()

        @pl.when(((core == 0) & (tok >= 2)) | ((core == 1) & (tok >= 4)))
        def _(which=which):
            across(2, 3, which).wait_send()

    for n in range(PEERS):
        out_copy(n).wait()
    pool_copy.wait()


def on_device(queries, key_states, value_states, query_gain, key_gain, lengths, slot_order):
    rows = queries.shape[0]
    shard = rows * PEERS
    slots = slot_order.shape[1]
    frequency = np.exp(np.arange(D // 2) * (-2.0 * math.log(1000000.0) / D)).astype(np.float32)
    frequency = jnp.asarray(np.concatenate([frequency, frequency])[None, :])
    vmem = pl.BlockSpec(memory_space=pltpu.VMEM)
    smem = pl.BlockSpec(memory_space=pltpu.SMEM)
    anywhere = pl.BlockSpec(memory_space=pl.ANY)
    bf16 = jnp.bfloat16
    dma = pltpu.SemaphoreType.DMA
    attention, pool = pl.pallas_call(
        functools.partial(kernel, lax.axis_size("tok")),
        out_shape=(
            jax.ShapeDtypeStruct((shard, GROUP * D), bf16),
            jax.ShapeDtypeStruct((slots * PAGE, 2 * D), bf16),
        ),
        in_specs=[anywhere, anywhere, anywhere, vmem, vmem, vmem, smem, vmem],
        out_specs=(anywhere, anywhere),
        scratch_shapes=[
            pltpu.VMEM((rows, PEERS * GROUP * D), bf16),
            pltpu.VMEM((rows, PEERS * D), bf16),
            pltpu.VMEM((rows, PEERS * D), bf16),
            pltpu.VMEM((PEERS, 2, rows, D), bf16),
            pltpu.VMEM((PEERS, GROUP * rows, D), bf16),
            pltpu.VMEM((2, (REACH + 1) * shard, D), bf16),
            pltpu.VMEM((PEERS, GROUP * rows, D), bf16),
            pltpu.VMEM((4, 2, rows, D), bf16),
            pltpu.VMEM((4, GROUP * rows, D), bf16),
            pltpu.VMEM((2, 2, shard // 2, D), bf16),
            pltpu.VMEM(((REACH + 1) * shard, D), bf16),
            pltpu.VMEM((shard, D), bf16),
            pltpu.VMEM((PEERS, GROUP * rows, D), jnp.float32),
            pltpu.VMEM((PEERS, GROUP * rows, D), jnp.float32),
            pltpu.VMEM((PEERS, GROUP * rows, D), jnp.float32),
            pltpu.VMEM((PEERS, rows, GROUP * D), bf16),
            pltpu.VMEM((slots * PAGE, 2 * D), bf16),
            dma((3,)),
            dma((3,)),
            dma((PEERS,)),
            dma((PEERS,)),
            dma((PEERS,)),
            dma((PEERS,)),
            dma((PEERS,)),
            dma((4,)),
            dma((4,)),
            dma((4,)),
            dma((4,)),
            dma((6,)),
            dma((4,)),
            dma((2,)),
            dma((2,)),
            dma((4,)),
            dma((4,)),
        ],
        compiler_params=pltpu.CompilerParams(
            collective_id=0, has_side_effects=True, vmem_limit_bytes=56 * 2**20
        ),
        name="paged_prefill",
    )(
        queries,
        key_states,
        value_states,
        query_gain[None, :],
        key_gain[None, :],
        frequency,
        lengths,
        slot_order,
    )
    return attention, pool.reshape(slots, PAGE, 1, 2 * D)


def solution(mesh):
    in_specs = (
        P(("tok", "head"), None),
        P(("tok", "head"), None),
        P(("tok", "head"), None),
        P(),
        P(),
        P(),
        P("tok", None),
    )
    out_specs = (P("tok", "head"), P("tok", None, "head", None))
    return jax.shard_map(
        on_device, mesh=mesh, in_specs=in_specs, out_specs=out_specs, check_vma=False
    )
```
